32 devices in a mesh: seq: 16 (over z, y, x), head: 2 (over core).
Axes of the slice: x: 2, y: 2, z: 4, core: 2. Of those that a mesh axis runs over, the one named last changes fastest.
Arguments:
- queries: bfloat16 [6144, 2048], P('seq', 'head'), may hold values from -6 to 6
- keys: bfloat16 [6144, 2048], P('seq', 'head'), may hold values from -0.5 to 0.5
- values: bfloat16 [6144, 2048], P('seq', 'head'), may hold values from -6 to 6
- level_pattern: int32 [6144], P('seq'), may hold values from 0 to 15
- level_weight: float32 [16, 9], replicated, may hold values from 0.5 to 2
- out_weight: bfloat16 [2, 1024, 2048], P('head', 'seq'), may hold values from -0.125 to 0.125
Outputs:
- mixed: float32 [6144, 2048], P('seq', 'head')
The draws below stay inside these ranges and needn't reach their ends.
All inputs are finite; a program needn't handle non-finite values.
Results may differ from the reference program's by a relative error of at most 0.003.
Values may be sent and summed in bfloat16 or wider, within the bound.
A program may use at most 64 MiB of HBM per device.

```python
import math
import jax
import jax.numpy as jnp
from jax import lax

D = 2048
HEADS = 16
HD = 128
LEVELS = 8
PATTERNS = 16
TOK_DEV = 384
TOKENS = 6144
N_SEQ = 16
N_HEAD = 2


def with_ends(result, stream_key, low, high):
    extent = result.shape
    index_at = [jax.random.randint(jax.random.fold_in(stream_key, axis), (), 0, extent[axis]) for axis in range(len(extent))]
    result = result.at[tuple(index_at)].set(low)
    longest = extent.index(max(extent))
    index_at[longest] = (index_at[longest] + 1) % extent[longest]
    return result.at[tuple(index_at)].set(high)


def levels(rng, shape, cuts, least, high):
    def one(position, shards_of):
        heights = jax.random.uniform(jax.random.fold_in(jax.random.fold_in(rng, 6), position), (shards_of,), jnp.float32, least / len(cuts), high / len(cuts))
        return jnp.repeat(jnp.exp(heights), shape[position] // shards_of).reshape((-1,) + (1,) * (len(shape) - position - 1))

    factor_of = one(*cuts[0])
    for cut in cuts[1:]:
        factor_of = factor_of * one(*cut)
    return factor_of


def centred(key, dims, deviation, limit, cuts=(), held_as=jnp.bfloat16):
    level = levels(key, dims, cuts, -0.22, 0.18) if cuts else 1.0
    drawn = jax.random.normal(key, dims, jnp.float32) * deviation * level
    return jnp.minimum(jnp.maximum(drawn, -limit), limit).astype(held_as)


def setup_inputs(seed: int = 0) -> dict:
    key_list = jax.random.split(jax.random.key(seed), 7)
    return {
        "queries": centred(key_list[0], (TOKENS, HEADS * HD), 1.0, 6.0, ((0, 16), (1, 2))),
        "keys": centred(key_list[1], (TOKENS, HEADS * HD), HD ** -0.5, 0.5, ((0, 16), (1, 2))),
        "values": centred(key_list[2], (TOKENS, HEADS * HD), 1.0, 6.0, ((0, 16), (1, 2))),
        "level_pattern": with_ends(jax.random.randint(key_list[3], (TOKENS,), 0, PATTERNS), jax.random.fold_in(key_list[3], 1), 0, PATTERNS - 1).astype(jnp.int32),
        "level_weight": jnp.clip(jnp.exp(jax.random.uniform(key_list[4], (PATTERNS, LEVELS + 1), jnp.float32, math.log(0.5), math.log(2.0))), 0.5, 2.0),
        "out_weight": centred(key_list[5], (N_HEAD, HEADS * HD // N_HEAD, D), (HEADS * HD) ** -0.5, 0.125, ((0, 2), (1, 16))),
    }


def reference(queries, keys, values, level_pattern, level_weight, out_weight):
    highest = lax.Precision.HIGHEST
    query = queries.reshape(N_SEQ, TOK_DEV, HEADS, HD).astype(jnp.float32)
    key_mat = keys.reshape(N_SEQ, TOK_DEV, HEADS, HD).astype(jnp.float32)
    value_mat = values.reshape(N_SEQ, TOK_DEV, HEADS, HD).astype(jnp.float32)
    scores = jnp.einsum('cthe,cshe->chts', query, key_mat, precision=highest)
    row_pos = lax.broadcasted_iota(jnp.int32, (TOK_DEV, TOK_DEV), 0)
    col_pos = lax.broadcasted_iota(jnp.int32, (TOK_DEV, TOK_DEV), 1)
    inner = jnp.where((col_pos <= row_pos)[None, None], scores, 0.0).astype(jnp.bfloat16)
    within = jnp.einsum('chts,cshf->cthf', inner.astype(jnp.float32), value_mat, precision=highest)
    within = within * (1.0 / math.sqrt(TOK_DEV))
    level_mix = level_weight[level_pattern].reshape(N_SEQ, TOK_DEV, LEVELS + 1)
    attended = level_mix[:, :, 0, None, None] * within
    states = jnp.einsum('cshe,cshf->chef', key_mat, value_mat, precision=highest)
    stretch_ids = jnp.arange(N_SEQ, dtype=jnp.int32)
    for level in range(LEVELS):
        span = 2 ** level
        if 2 * span > N_SEQ:
            break
        blocks = states.reshape(N_SEQ // span, span, HEADS, HD, HD).sum(axis=1)
        partner = blocks[jnp.bitwise_xor(stretch_ids // span, 1).astype(jnp.int32)]
        active = (stretch_ids // span % 2 == 1).astype(jnp.float32)
        level_read = jnp.einsum('cthe,chef->cthf', query, partner, precision=highest)
        factor = 1.0 / math.sqrt(span * TOK_DEV)
        coef = level_mix[:, :, level + 1] * active[:, None] * factor
        attended = attended + coef[:, :, None, None] * level_read
    attended = attended.reshape(TOKENS, HEADS * HD).astype(jnp.bfloat16)
    projection = out_weight.reshape(HEADS * HD, D)
    return jnp.dot(attended, projection, preferred_element_type=jnp.float32)
```

```python
import functools
import itertools
import math

import jax
import jax.numpy as jnp
from jax import lax
from jax.experimental import pallas as pl
from jax.experimental.pallas import tpu as pltpu
from jax.sharding import PartitionSpec as P

HD = 128
MESH = pl.DeviceIdType.MESH


def line_dims(mesh):
    n = mesh.shape["seq"]
    devices = mesh.devices.reshape(n, -1)[:, 0]
    coords = [tuple(getattr(d, "coords", ())) for d in devices]
    dims = []
    if len(set(coords)) == n:
        for axis in range(len(coords[0])):
            seen = [c[axis] - coords[0][axis] for c in coords]
            length = max(seen) + 1
            if length > 1:
                dims.append((length, seen.index(1)))
    stride = 1
    for length, step in sorted(dims, key=lambda d: d[1]):
        if step != stride:
            break
        stride *= length
    if not dims or stride != n:
        dims = [(2, 1 << i) for i in range(n.bit_length() - 1)]
    return sorted(dims, key=lambda d: -d[1])


def nearest(k, p, n):
    m = jnp.minimum(p, n - 1 - p)
    sign = jnp.where(p == m, 1, -1)
    near = (k + 1) // 2 * (2 * (k % 2) - 1)
    if n == 2:
        return p + k * (1 - 2 * p)
    return jnp.where(k <= 2 * m, p + near, p + sign * (k - m))


def kernel(
    plan, q_hbm, k_hbm, v_hbm, pattern_ref, table_ref, w_hbm, *rest
):
    dims, orders, cuts, events, n, fused = plan
    if fused:
        out_ref, *rest = rest
    else:
        att_hbm, w_out_hbm, *rest = rest
    (q_ref, k_ref, v_ref, w_ref, wbuf, att, acc, sub, outgoing, incoming, mixb,
     load_sem, own_sem, pair_send, pair_recv, w_send, w_recv, s_send, s_recv, a_send, a_recv) = rest
    me = lax.axis_index("seq")
    core = lax.axis_index("head")
    other = 1 - core
    tokens, width = q_ref.shape
    heads = width // HD
    cols = wbuf.shape[-1]
    bits = n.bit_length() - 1
    groups = a_send.shape[0]
    per = heads // groups
    place = [me // stride % length for length, stride in dims]

    loads = [
        pltpu.make_async_copy(src, dst, load_sem.at[i])
        for i, (src, dst) in enumerate(((w_hbm, w_ref), (k_hbm, k_ref), (v_hbm, v_ref), (q_hbm, q_ref)))
    ]
    for load in loads:
        load.start()

    barrier = pltpu.get_barrier_semaphore()
    total = 1
    pl.semaphore_signal(barrier, inc=1, device_id=(me, other), device_id_type=MESH)
    for bit in range(bits):
        pl.semaphore_signal(barrier, inc=1, device_id=(me ^ (1 << bit), core), device_id_type=MESH)
        total += 1
    for (length, stride), p in zip(dims, place):
        if length == 2:
            continue
        for step in (-1, 1):
            there = jnp.logical_and(p + step >= 0, p + step < length)

            @pl.when(there)
            def _():
                pl.semaphore_signal(barrier, inc=1, device_id=(me + step * stride, core), device_id_type=MESH)

            total = total + there.astype(jnp.int32)

    for l in range(bits + 1):
        if l == 0:
            ids = lax.broadcasted_iota(jnp.int32, (table_ref.shape[0], tokens), 0)
            one_hot = (ids == pattern_ref[...]).astype(jnp.float32)
            mix = lax.dot_general(
                one_hot, table_ref[...], (((0,), (0,)), ((), ())),
                precision=lax.Precision.HIGHEST, preferred_element_type=jnp.float32,
            )
        factor = 1.0 / math.sqrt(tokens * (1 if l == 0 else 2 ** (l - 1)))
        mixb[l] = jnp.broadcast_to(mix[:, l : l + 1] * factor, (tokens, HD))

    def head_cols(h):
        return slice(h * HD, (h + 1) * HD)

    loads[1].wait()
    loads[2].wait()

    def make_states(h):
        state = lax.dot_general(
            k_ref[:, head_cols(h)], v_ref[:, head_cols(h)], (((0,), (0,)), ((), ())),
            preferred_element_type=jnp.float32,
        )
        sub[h] = state
        outgoing[0, h] = state.astype(jnp.bfloat16)

    for h in range(heads):
        make_states(h)
    loads[0].wait()
    pl.semaphore_wait(barrier, total)

    def pair_copy():
        return pltpu.make_async_remote_copy(
            src_ref=w_ref.at[0, :, pl.ds(pl.multiple_of(other * cols, 128), cols)],
            dst_ref=wbuf.at[core, me], send_sem=pair_send, recv_sem=pair_recv,
            device_id=(me, other), device_id_type=MESH,
        )

    def pair_landed():
        return pltpu.make_async_remote_copy(
            src_ref=w_ref.at[0, :, pl.ds(pl.multiple_of(other * cols, 128), cols)],
            dst_ref=wbuf.at[other, me], send_sem=pair_send, recv_sem=pair_recv,
            device_id=(me, other), device_id_type=MESH,
        )

    pair_copy().start()
    own = pltpu.make_async_copy(
        w_ref.at[0, :, pl.ds(pl.multiple_of(core * cols, 128), cols)], wbuf.at[core, me], own_sem
    )
    own.start()

    def state_copy(level, group):
        piece = pl.ds(group * per, per)
        return pltpu.make_async_remote_copy(
            src_ref=outgoing.at[level, piece], dst_ref=incoming.at[level, piece],
            send_sem=s_send.at[level, group], recv_sem=s_recv.at[level, group],
            device_id=(me ^ (1 << level), core), device_id_type=MESH,
        )

    def sum_needed(level):
        return me // 2 ** (level + 1) != n // 2 ** (level + 1) - 1

    def active(level):
        return me // 2**level % 2 == 1

    def sends(level):
        return jnp.logical_or(jnp.logical_not(active(level)), sum_needed(level))

    def receives(level):
        return jnp.logical_or(active(level), sum_needed(level))

    for group in range(groups):
        @pl.when(sends(0))
        def _():
            state_copy(0, group).start()

    def weight_copy(part, source, slot, target):
        lo, size = cuts[part]
        piece = wbuf.at[:, source, :, pl.ds(lo, size)]
        return pltpu.make_async_remote_copy(
            src_ref=piece, dst_ref=piece,
            send_sem=w_send.at[part, source if fused else 0, slot], recv_sem=w_recv.at[part, source],
            device_id=(target, core), device_id_type=MESH,
        )

    def forward(part, source, at, arrived, action):
        order = orders[part]
        for rank in range(max(arrived, 0), len(order)):
            d = order[rank]
            length, stride = dims[d]
            for slot, step in ((2 * rank, 1), (2 * rank + 1, -1)):
                if rank == arrived and length == 2:
                    continue
                ok = jnp.logical_and(place[d] + step >= 0, place[d] + step < length)
                if rank == arrived:
                    ok = jnp.logical_and(ok, (place[d] - at[d]) * step > 0)

                @pl.when(ok)
                def _():
                    copy = weight_copy(part, source, slot, me + step * stride)
                    if action == "start":
                        copy.start()
                    else:
                        copy.wait_send()

    def source_of(part, ks):
        at = {d: nearest(k, place[d], dims[d][0]) for d, k in zip(orders[part], ks)}
        return at, sum(at[d] * dims[d][1] for d in at)

    def arrived_by(ks):
        return max((r for r, k in enumerate(ks) if k), default=-1)

    def weight_event(part, ks, arrived):
        at, source = source_of(part, ks)
        weight_copy(part, source, 0, me).wait_recv()
        forward(part, source, at, arrived, "start")
        if not fused:
            forward(part, source, at, arrived, "wait")

    def read_state(level, h):
        acc[:, head_cols(h)] += mixb[level + 1] * jnp.dot(
            q_ref[:, head_cols(h)], incoming[level, h], preferred_element_type=jnp.float32
        )

    def within_event(h):
        columns = head_cols(h)
        scores = lax.dot_general(
            q_ref[:, columns], k_ref[:, columns], (((1,), (1,)), ((), ())),
            preferred_element_type=jnp.float32,
        )
        row = lax.broadcasted_iota(jnp.int32, (tokens, tokens), 0)
        col = lax.broadcasted_iota(jnp.int32, (tokens, tokens), 1)
        inner = jnp.where(col <= row, scores, 0.0).astype(jnp.bfloat16)
        acc[:, columns] = mixb[0] * jnp.dot(inner, v_ref[:, columns], preferred_element_type=jnp.float32)

    def att_copy(group, mine):
        columns = pl.ds(group * per * HD, per * HD)
        which = core if mine else other
        return pltpu.make_async_remote_copy(
            src_ref=att.at[core, :, columns], dst_ref=att.at[which, :, columns],
            send_sem=a_send.at[group], recv_sem=a_recv.at[group],
            device_id=(me, other), device_id_type=MESH,
        )

    def state_event(level, group):
        @pl.when(receives(level))
        def _():
            state_copy(level, group).wait_recv()

        span = range(group * per, (group + 1) * per)
        if level + 1 < bits:
            @pl.when(sum_needed(level))
            def _():
                for h in span:
                    summed = sub[h] + incoming[level, h].astype(jnp.float32)
                    sub[h] = summed
                    outgoing[level + 1, h] = summed.astype(jnp.bfloat16)

            @pl.when(sends(level + 1))
            def _():
                state_copy(level + 1, group).start()

        @pl.when(active(level))
        def _():
            for h in span:
                read_state(level, h)

        if level + 1 == bits:
            columns = slice(group * per * HD, (group + 1) * per * HD)
            att[core, :, columns] = acc[:, columns].astype(jnp.bfloat16)
            att_copy(group, True).start()

    own.wait()
    pair_landed().wait_recv()
    for part in range(len(orders)):
        at, source = source_of(part, (0,) * len(dims))
        forward(part, source, at, -1, "start")
        if not fused:
            forward(part, source, at, -1, "wait")
    loads[3].wait()

    def project(part):
        lo, size = cuts[part]
        columns = slice(lo, lo + size)
        flat = [wbuf[g, :, :, columns].reshape(-1, size) for g in range(2)]
        out_ref[:, columns] = jnp.dot(att[0], flat[0], preferred_element_type=jnp.float32) + jnp.dot(
            att[1], flat[1], preferred_element_type=jnp.float32
        )

    for event in events:
        if event[0] == "within":
            within_event(event[1])
        elif event[0] == "state":
            state_event(event[1], event[2])
        elif event[0] == "weight":
            weight_event(*event[1:])
        elif event[0] == "loop":
            lengths = [[dims[d][0] for d in order] for order in orders]

            def each(e, carry):
                for part, order in enumerate(orders):
                    for arrived in range(len(order)):
                        below = math.prod(lengths[part][:arrived])
                        ks = []
                        rest_e = e
                        for length in lengths[part]:
                            ks.append(rest_e % length)
                            rest_e = rest_e // length

                        @pl.when(jnp.logical_and(e >= below, e < below * lengths[part][arrived]))
                        def _():
                            weight_event(part, ks, arrived)

                return carry

            lax.fori_loop(1, n, each, 0)
        elif event[0] == "att":
            for group in range(groups):
                att_copy(group, False).wait_recv()
        elif event[0] == "project" and fused:
            project(event[1])

    def finish(part, e):
        ks = []
        for d in orders[part]:
            ks.append(e % dims[d][0])
            e = e // dims[d][0]
        return ks

    pair_copy().wait_send()
    for group in range(groups):
        att_copy(group, True).wait_send()
        for level in range(bits):
            @pl.when(sends(level))
            def _():
                state_copy(level, group).wait_send()
    if fused:
        for part in range(len(orders)):
            for e in range(n):
                ks = finish(part, e)
                at, source = source_of(part, ks)
                forward(part, source, at, arrived_by(ks), "wait")
    if not fused:
        stores = [pltpu.make_async_copy(att, att_hbm, load_sem.at[0]), pltpu.make_async_copy(wbuf, w_out_hbm, load_sem.at[1])]
        for store in stores:
            store.start()
        for store in stores:
            store.wait()


def schedule(dims, orders, cuts, n, heads, groups, unrolled):
    bits = n.bit_length() - 1
    whole = sum(size for _, size in cuts)
    timed = []
    for h in range(heads):
        timed.append((0.35 * h / heads, ("within", h)))
    for level in range(bits):
        for group in range(groups):
            timed.append((0.45 + 0.75 * level + 0.25 * group, ("state", level, group)))
    if not unrolled:
        tail = [("loop",), ("att",)]
    else:
        last = {}
        for part, order in enumerate(orders):
            lengths = [dims[d][0] for d in order]
            count = [0] * len(order)
            for rev in itertools.product(*[range(length) for length in lengths[::-1]]):
                ks = rev[::-1]
                arrived = max((r for r, k in enumerate(ks) if k), default=-1)
                if arrived < 0:
                    continue
                count[arrived] += 1
                when = count[arrived] * cuts[part][1] / whole * 1.8 + 0.3 * sum(1 for k in ks if k)
                if arrived == len(order) - 1 and lengths[-1] == 2:
                    when += 100
                timed.append((when, ("weight", part, ks, arrived)))
        tail = [("att",)]
    timed.sort(key=lambda t: t[0])
    return [e for _, e in timed] + tail + [("project", p) for p in range(len(orders))]


def on_device(dims, queries, keys, values, level_pattern, level_weight, out_weight):
    n = lax.axis_size("seq")
    tokens, width = queries.shape
    heads = width // HD
    bits = n.bit_length() - 1
    _, rows, full = out_weight.shape
    cols = full // 2
    fused = rows % 16 == 0
    groups = min(4, heads)
    tiles = cols // 128
    if len(dims) == 3:
        long = max(range(3), key=lambda i: dims[i][0])
        a, b = [i for i in range(3) if i != long]
        orders = [(long, a, b), (long, b, a), (a, b, long)]
        share = max(1, tiles * 3 // 8)
        sizes = [share, share, tiles - 2 * share]
    else:
        orders, sizes = [tuple(range(len(dims)))], [tiles]
    cuts, lo = [], 0
    for size in sizes:
        cuts.append((lo * 128, size * 128))
        lo += size
    events = schedule(dims, orders, cuts, n, heads, groups, fused)
    plan = (dims, orders, cuts, events, n, fused)
    bf16, f32 = jnp.bfloat16, jnp.float32
    any_spec = pl.BlockSpec(memory_space=pl.ANY)
    vmem_spec = pl.BlockSpec(memory_space=pltpu.VMEM)
    if fused:
        out_shape = jax.ShapeDtypeStruct((tokens, cols), f32)
        out_specs = vmem_spec
    else:
        out_shape = [
            jax.ShapeDtypeStruct((2, tokens, width), bf16),
            jax.ShapeDtypeStruct((2, n, rows, cols), bf16),
        ]
        out_specs = [any_spec, any_spec]
    dma = pltpu.SemaphoreType.DMA
    result = pl.pallas_call(
        functools.partial(kernel, plan),
        out_shape=out_shape,
        in_specs=[any_spec] * 3 + [vmem_spec] * 2 + [any_spec],
        out_specs=out_specs,
        scratch_shapes=[
            pltpu.VMEM((tokens, width), bf16),
            pltpu.VMEM((tokens, width), bf16),
            pltpu.VMEM((tokens, width), bf16),
            pltpu.VMEM((1, rows, full), bf16),
            pltpu.VMEM((2, n, rows, cols), bf16),
            pltpu.VMEM((2, tokens, width), bf16),
            pltpu.VMEM((tokens, width), f32),
            pltpu.VMEM((heads, HD, HD), f32),
            pltpu.VMEM((bits, heads, HD, HD), bf16),
            pltpu.VMEM((bits, heads, HD, HD), bf16),
            pltpu.VMEM((bits + 1, tokens, HD), f32),
            dma((4,)),
            dma,
            dma,
            dma,
            dma((len(orders), n if fused else 1, 2 * len(dims))),
            dma((len(orders), n)),
            dma((bits, groups)),
            dma((bits, groups)),
            dma((groups,)),
            dma((groups,)),
        ],
        compiler_params=pltpu.CompilerParams(
            collective_id=0, has_side_effects=True, vmem_limit_bytes=60 * 2**20
        ),
    )(queries, keys, values, level_pattern.reshape(1, tokens), level_weight, out_weight)
    if fused:
        return result
    att, gathered = result
    return jnp.einsum(
        "gtk,gkd->td", att, gathered.reshape(2, n * rows, cols), preferred_element_type=f32
    )


def solution(mesh):
    placed = (
        P("seq", "head"),
        P("seq", "head"),
        P("seq", "head"),
        P("seq"),
        P(),
        P("head", "seq", None),
    )
    return jax.shard_map(
        functools.partial(on_device, line_dims(mesh)),
        mesh=mesh, in_specs=placed, out_specs=P("seq", "head"), check_vma=False,
    )
```

```python
import functools
import itertools
import math

import jax
import jax.numpy as jnp
from jax import lax
from jax.experimental import pallas as pl
from jax.experimental.pallas import tpu as pltpu
from jax.sharding import PartitionSpec as P

HD = 128
MESH = pl.DeviceIdType.MESH


def line_dims(mesh):
    n = mesh.shape["seq"]
    devices = mesh.devices.reshape(n, -1)[:, 0]
    coords = [tuple(getattr(d, "coords", ())) for d in devices]
    dims = []
    if len(set(coords)) == n:
        for axis in range(len(coords[0])):
            seen = [c[axis] - coords[0][axis] for c in coords]
            length = max(seen) + 1
            if length > 1:
                dims.append((length, seen.index(1)))
    stride = 1
    for length, step in sorted(dims, key=lambda d: d[1]):
        if step != stride:
            break
        stride *= length
    if not dims or stride != n:
        dims = [(2, 1 << i) for i in range(n.bit_length() - 1)]
    return sorted(dims, key=lambda d: -d[1])


def nearest(k, p, n):
    m = jnp.minimum(p, n - 1 - p)
    sign = jnp.where(p == m, 1, -1)
    near = (k + 1) // 2 * (2 * (k % 2) - 1)
    if n == 2:
        return p + k * (1 - 2 * p)
    return jnp.where(k <= 2 * m, p + near, p + sign * (k - m))


def kernel(
    plan, q_hbm, k_hbm, v_hbm, pattern_ref, table_ref, w_hbm, *rest
):
    dims, orders, cuts, events, n, fused = plan
    if fused:
        out_ref, *rest = rest
    else:
        att_hbm, w_out_hbm, *rest = rest
    (q_ref, k_ref, v_ref, w_ref, wbuf, att, acc, sub, outgoing, incoming, scale_out, scale_in, mixb,
     load_sem, own_sem, pair_send, pair_recv, w_send, w_recv, s_send, s_recv, t_send, t_recv, a_send, a_recv) = rest
    me = lax.axis_index("seq")
    core = lax.axis_index("head")
    other = 1 - core
    tokens, width = q_ref.shape
    heads = width // HD
    cols = wbuf.shape[-1]
    bits = n.bit_length() - 1
    groups = a_send.shape[0]
    per = heads // groups
    place = [me // stride % length for length, stride in dims]

    loads = [
        pltpu.make_async_copy(src, dst, load_sem.at[i])
        for i, (src, dst) in enumerate(((w_hbm, w_ref), (k_hbm, k_ref), (v_hbm, v_ref), (q_hbm, q_ref)))
    ]
    for load in loads:
        load.start()

    barrier = pltpu.get_barrier_semaphore()
    total = 1
    pl.semaphore_signal(barrier, inc=1, device_id=(me, other), device_id_type=MESH)
    for bit in range(bits):
        pl.semaphore_signal(barrier, inc=1, device_id=(me ^ (1 << bit), core), device_id_type=MESH)
        total += 1
    for (length, stride), p in zip(dims, place):
        if length == 2:
            continue
        for step in (-1, 1):
            there = jnp.logical_and(p + step >= 0, p + step < length)

            @pl.when(there)
            def _():
                pl.semaphore_signal(barrier, inc=1, device_id=(me + step * stride, core), device_id_type=MESH)

            total = total + there.astype(jnp.int32)

    for l in range(bits + 1):
        if l == 0:
            ids = lax.broadcasted_iota(jnp.int32, (table_ref.shape[0], tokens), 0)
            one_hot = (ids == pattern_ref[...].reshape(1, tokens)).astype(jnp.float32)
            mix = lax.dot_general(
                one_hot, table_ref[...], (((0,), (0,)), ((), ())),
                precision=lax.Precision.HIGHEST, preferred_element_type=jnp.float32,
            )
        factor = 1.0 / math.sqrt(tokens * (1 if l == 0 else 2 ** (l - 1)))
        mixb[l] = jnp.broadcast_to(mix[:, l : l + 1] * factor, (tokens, HD))

    def head_cols(h):
        return slice(h * HD, (h + 1) * HD)

    loads[1].wait()
    loads[2].wait()

    def pack_state(level, h, state):
        top = jnp.maximum(jnp.max(jnp.abs(state), axis=0, keepdims=True), 1e-30)
        scaled = jnp.round(state * (32767.0 / top))
        outgoing[level, h] = scaled.astype(jnp.int32).astype(jnp.int16)
        scale_out[level, h] = jnp.broadcast_to(top * (1.0 / 32767.0), (8, HD))

    def unpack_state(level, h):
        return incoming[level, h].astype(jnp.int32).astype(jnp.float32) * scale_in[level, h, 0:1]

    def make_states(h):
        state = lax.dot_general(
            k_ref[:, head_cols(h)], v_ref[:, head_cols(h)], (((0,), (0,)), ((), ())),
            preferred_element_type=jnp.float32,
        )
        sub[h] = state
        pack_state(0, h, state)

    for h in range(heads):
        make_states(h)
    loads[0].wait()
    pl.semaphore_wait(barrier, total)

    def pair_copy():
        return pltpu.make_async_remote_copy(
            src_ref=w_ref.at[0, :, pl.ds(pl.multiple_of(other * cols, 128), cols)],
            dst_ref=wbuf.at[core, me], send_sem=pair_send, recv_sem=pair_recv,
            device_id=(me, other), device_id_type=MESH,
        )

    def pair_landed():
        return pltpu.make_async_remote_copy(
            src_ref=w_ref.at[0, :, pl.ds(pl.multiple_of(other * cols, 128), cols)],
            dst_ref=wbuf.at[other, me], send_sem=pair_send, recv_sem=pair_recv,
            device_id=(me, other), device_id_type=MESH,
        )

    pair_copy().start()
    own = pltpu.make_async_copy(
        w_ref.at[0, :, pl.ds(pl.multiple_of(core * cols, 128), cols)], wbuf.at[core, me], own_sem
    )
    own.start()

    def state_copy(level, group):
        piece = pl.ds(group * per, per)
        return pltpu.make_async_remote_copy(
            src_ref=outgoing.at[level, piece], dst_ref=incoming.at[level, piece],
            send_sem=s_send.at[level, group], recv_sem=s_recv.at[level, group],
            device_id=(me ^ (1 << level), core), device_id_type=MESH,
        )

    def scale_copy(level, group):
        piece = pl.ds(group * per, per)
        return pltpu.make_async_remote_copy(
            src_ref=scale_out.at[level, piece], dst_ref=scale_in.at[level, piece],
            send_sem=t_send.at[level, group], recv_sem=t_recv.at[level, group],
            device_id=(me ^ (1 << level), core), device_id_type=MESH,
        )

    def sum_needed(level):
        return me // 2 ** (level + 1) != n // 2 ** (level + 1) - 1

    def active(level):
        return me // 2**level % 2 == 1

    def sends(level):
        return jnp.logical_or(jnp.logical_not(active(level)), sum_needed(level))

    def receives(level):
        return jnp.logical_or(active(level), sum_needed(level))

    for group in range(groups):
        @pl.when(sends(0))
        def _():
            scale_copy(0, group).start()
            state_copy(0, group).start()

    def weight_copy(part, source, slot, target):
        lo, size = cuts[part]
        piece = wbuf.at[:, source, :, pl.ds(lo, size)]
        return pltpu.make_async_remote_copy(
            src_ref=piece, dst_ref=piece,
            send_sem=w_send.at[part, source if fused else 0, slot], recv_sem=w_recv.at[part, source],
            device_id=(target, core), device_id_type=MESH,
        )

    def forward(part, source, at, arrived, action):
        order = orders[part]
        for rank in range(max(arrived, 0), len(order)):
            d = order[rank]
            length, stride = dims[d]
            for slot, step in ((2 * rank, 1), (2 * rank + 1, -1)):
                if rank == arrived and length == 2:
                    continue
                ok = jnp.logical_and(place[d] + step >= 0, place[d] + step < length)
                if rank == arrived:
                    ok = jnp.logical_and(ok, (place[d] - at[d]) * step > 0)

                @pl.when(ok)
                def _():
                    copy = weight_copy(part, source, slot, me + step * stride)
                    if action == "start":
                        copy.start()
                    else:
                        copy.wait_send()

    def source_of(part, ks):
        at = {d: nearest(k, place[d], dims[d][0]) for d, k in zip(orders[part], ks)}
        return at, sum(at[d] * dims[d][1] for d in at)

    def arrived_by(ks):
        return max((r for r, k in enumerate(ks) if k), default=-1)

    def weight_event(part, ks, arrived):
        at, source = source_of(part, ks)
        weight_copy(part, source, 0, me).wait_recv()
        forward(part, source, at, arrived, "start")
        if not fused:
            forward(part, source, at, arrived, "wait")

    def read_state(level, h):
        block = unpack_state(level, h)
        high = block.astype(jnp.bfloat16)
        low = (block - high.astype(jnp.float32)).astype(jnp.bfloat16)
        query = q_ref[:, head_cols(h)]
        acc[:, head_cols(h)] += mixb[level + 1] * (
            jnp.dot(query, high, preferred_element_type=jnp.float32)
            + jnp.dot(query, low, preferred_element_type=jnp.float32)
        )

    def within_event(h):
        columns = head_cols(h)
        scores = lax.dot_general(
            q_ref[:, columns], k_ref[:, columns], (((1,), (1,)), ((), ())),
            preferred_element_type=jnp.float32,
        )
        row = lax.broadcasted_iota(jnp.int32, (tokens, tokens), 0)
        col = lax.broadcasted_iota(jnp.int32, (tokens, tokens), 1)
        inner = jnp.where(col <= row, scores, 0.0).astype(jnp.bfloat16)
        acc[:, columns] = mixb[0] * jnp.dot(inner, v_ref[:, columns], preferred_element_type=jnp.float32)

    def att_copy(group, mine):
        columns = pl.ds(group * per * HD, per * HD)
        which = core if mine else other
        return pltpu.make_async_remote_copy(
            src_ref=att.at[core, :, columns], dst_ref=att.at[which, :, columns],
            send_sem=a_send.at[group], recv_sem=a_recv.at[group],
            device_id=(me, other), device_id_type=MESH,
        )

    def state_event(level, group):
        @pl.when(receives(level))
        def _():
            scale_copy(level, group).wait_recv()
            state_copy(level, group).wait_recv()

        span = range(group * per, (group + 1) * per)
        if level + 1 < bits:
            @pl.when(sum_needed(level))
            def _():
                for h in span:
                    summed = sub[h] + unpack_state(level, h)
                    sub[h] = summed
                    pack_state(level + 1, h, summed)

            @pl.when(sends(level + 1))
            def _():
                scale_copy(level + 1, group).start()
                state_copy(level + 1, group).start()

        @pl.when(active(level))
        def _():
            for h in span:
                read_state(level, h)

        if level + 1 == bits:
            columns = slice(group * per * HD, (group + 1) * per * HD)
            att[core, :, columns] = acc[:, columns].astype(jnp.bfloat16)
            att_copy(group, True).start()

    own.wait()
    pair_landed().wait_recv()
    for part in range(len(orders)):
        at, source = source_of(part, (0,) * len(dims))
        forward(part, source, at, -1, "start")
        if not fused:
            forward(part, source, at, -1, "wait")
    loads[3].wait()

    def project(part):
        lo, size = cuts[part]
        columns = slice(lo, lo + size)
        flat = [wbuf[g, :, :, columns].reshape(-1, size) for g in range(2)]
        out_ref[:, columns] = jnp.dot(att[0], flat[0], preferred_element_type=jnp.float32) + jnp.dot(
            att[1], flat[1], preferred_element_type=jnp.float32
        )

    for event in events:
        if event[0] == "within":
            within_event(event[1])
        elif event[0] == "state":
            state_event(event[1], event[2])
        elif event[0] == "weight":
            weight_event(*event[1:])
        elif event[0] == "loop":
            lengths = [[dims[d][0] for d in order] for order in orders]

            def each(e, carry):
                for part, order in enumerate(orders):
                    for arrived in range(len(order)):
                        below = math.prod(lengths[part][:arrived])
                        ks = []
                        rest_e = e
                        for length in lengths[part]:
                            ks.append(rest_e % length)
                            rest_e = rest_e // length

                        @pl.when(jnp.logical_and(e >= below, e < below * lengths[part][arrived]))
                        def _():
                            weight_event(part, ks, arrived)

                return carry

            lax.fori_loop(1, n, each, 0)
        elif event[0] == "att":
            for group in range(groups):
                att_copy(group, False).wait_recv()
        elif event[0] == "project" and fused:
            project(event[1])

    def finish(part, e):
        ks = []
        for d in orders[part]:
            ks.append(e % dims[d][0])
            e = e // dims[d][0]
        return ks

    pair_copy().wait_send()
    for group in range(groups):
        att_copy(group, True).wait_send()
        for level in range(bits):
            @pl.when(sends(level))
            def _():
                scale_copy(level, group).wait_send()
                state_copy(level, group).wait_send()
    if fused:
        for part in range(len(orders)):
            for e in range(n):
                ks = finish(part, e)
                at, source = source_of(part, ks)
                forward(part, source, at, arrived_by(ks), "wait")
    if not fused:
        stores = [pltpu.make_async_copy(att, att_hbm, load_sem.at[0]), pltpu.make_async_copy(wbuf, w_out_hbm, load_sem.at[1])]
        for store in stores:
            store.start()
        for store in stores:
            store.wait()


def schedule(dims, orders, cuts, n, heads, groups, unrolled):
    bits = n.bit_length() - 1
    whole = sum(size for _, size in cuts)
    timed = []
    for h in range(heads):
        timed.append((0.35 * h / heads, ("within", h)))
    for level in range(bits):
        for group in range(groups):
            timed.append((0.45 + 0.75 * level + 0.25 * group, ("state", level, group)))
    if not unrolled:
        tail = [("loop",), ("att",)]
    else:
        last = {}
        for part, order in enumerate(orders):
            lengths = [dims[d][0] for d in order]
            count = [0] * len(order)
            for rev in itertools.product(*[range(length) for length in lengths[::-1]]):
                ks = rev[::-1]
                arrived = max((r for r, k in enumerate(ks) if k), default=-1)
                if arrived < 0:
                    continue
                count[arrived] += 1
                when = count[arrived] * cuts[part][1] / whole * 1.8 + 0.3 * sum(1 for k in ks if k)
                if arrived == len(order) - 1 and lengths[-1] == 2:
                    when += 100
                timed.append((when, ("weight", part, ks, arrived)))
        tail = [("att",)]
    timed.sort(key=lambda t: t[0])
    return [e for _, e in timed] + tail + [("project", p) for p in range(len(orders))]


def on_device(dims, queries, keys, values, level_pattern, level_weight, out_weight):
    n = lax.axis_size("seq")
    tokens, width = queries.shape
    heads = width // HD
    bits = n.bit_length() - 1
    _, rows, full = out_weight.shape
    cols = full // 2
    fused = rows % 16 == 0
    groups = min(4, heads)
    tiles = cols // 128
    if len(dims) == 3:
        long = max(range(3), key=lambda i: dims[i][0])
        a, b = [i for i in range(3) if i != long]
        orders = [(long, a, b), (long, b, a), (a, b, long)]
        share = max(1, tiles * 3 // 8)
        sizes = [share, share, tiles - 2 * share]
    else:
        orders, sizes = [tuple(range(len(dims)))], [tiles]
    cuts, lo = [], 0
    for size in sizes:
        cuts.append((lo * 128, size * 128))
        lo += size
    events = schedule(dims, orders, cuts, n, heads, groups, fused)
    plan = (dims, orders, cuts, events, n, fused)
    bf16, f32 = jnp.bfloat16, jnp.float32
    any_spec = pl.BlockSpec(memory_space=pl.ANY)
    vmem_spec = pl.BlockSpec(memory_space=pltpu.VMEM)
    if fused:
        out_shape = jax.ShapeDtypeStruct((tokens, cols), f32)
        out_specs = vmem_spec
    else:
        out_shape = [
            jax.ShapeDtypeStruct((2, tokens, width), bf16),
            jax.ShapeDtypeStruct((2, n, rows, cols), bf16),
        ]
        out_specs = [any_spec, any_spec]
    dma = pltpu.SemaphoreType.DMA
    result = pl.pallas_call(
        functools.partial(kernel, plan),
        out_shape=out_shape,
        in_specs=[any_spec] * 3 + [vmem_spec] * 2 + [any_spec],
        out_specs=out_specs,
        scratch_shapes=[
            pltpu.VMEM((tokens, width), bf16),
            pltpu.VMEM((tokens, width), bf16),
            pltpu.VMEM((tokens, width), bf16),
            pltpu.VMEM((1, rows, full), bf16),
            pltpu.VMEM((2, n, rows, cols), bf16),
            pltpu.VMEM((2, tokens, width), bf16),
            pltpu.VMEM((tokens, width), f32),
            pltpu.VMEM((heads, HD, HD), f32),
            pltpu.VMEM((bits, heads, HD, HD), jnp.int16),
            pltpu.VMEM((bits, heads, HD, HD), jnp.int16),
            pltpu.VMEM((bits, heads, 8, HD), f32),
            pltpu.VMEM((bits, heads, 8, HD), f32),
            pltpu.VMEM((bits + 1, tokens, HD), f32),
            dma((4,)),
            dma,
            dma,
            dma,
            dma((len(orders), n if fused else 1, 2 * len(dims))),
            dma((len(orders), n)),
            dma((bits, groups)),
            dma((bits, groups)),
            dma((bits, groups)),
            dma((bits, groups)),
            dma((groups,)),
            dma((groups,)),
        ],
        compiler_params=pltpu.CompilerParams(
            collective_id=0, has_side_effects=True, vmem_limit_bytes=60 * 2**20
        ),
    )(queries, keys, values, level_pattern, level_weight, out_weight)
    if fused:
        return result
    att, gathered = result
    return jnp.einsum(
        "gtk,gkd->td", att, gathered.reshape(2, n * rows, cols), preferred_element_type=f32
    )


def solution(mesh):
    placed = (
        P("seq", "head"),
        P("seq", "head"),
        P("seq", "head"),
        P("seq"),
        P(),
        P("head", "seq", None),
    )
    return jax.shard_map(
        functools.partial(on_device, line_dims(mesh)),
        mesh=mesh, in_specs=placed, out_specs=P("seq", "head"), check_vma=False,
    )
```

```python
import functools
import itertools
import math

import jax
import jax.numpy as jnp
from jax import lax
from jax.experimental import pallas as pl
from jax.experimental.pallas import tpu as pltpu
from jax.sharding import PartitionSpec as P

HD = 128
MESH = pl.DeviceIdType.MESH


def line_dims(mesh):
    n = mesh.shape["seq"]
    devices = mesh.devices.reshape(n, -1)[:, 0]
    coords = [tuple(getattr(d, "coords", ())) for d in devices]
    dims = []
    if len(set(coords)) == n:
        for axis in range(len(coords[0])):
            seen = [c[axis] - coords[0][axis] for c in coords]
            length = max(seen) + 1
            if length > 1:
                dims.append((length, seen.index(1)))
    stride = 1
    for length, step in sorted(dims, key=lambda d: d[1]):
        if step != stride:
            break
        stride *= length
    if not dims or stride != n:
        dims = [(2, 1 << i) for i in range(n.bit_length() - 1)]
    return sorted(dims, key=lambda d: -d[1])


def nearest(k, p, n):
    m = jnp.minimum(p, n - 1 - p)
    sign = jnp.where(p == m, 1, -1)
    near = (k + 1) // 2 * (2 * (k % 2) - 1)
    if n == 2:
        return p + k * (1 - 2 * p)
    return jnp.where(k <= 2 * m, p + near, p + sign * (k - m))


def kernel(
    plan, q_hbm, k_hbm, v_hbm, pattern_ref, table_ref, w_hbm, *rest
):
    dims, orders, cuts, events, n, fused = plan
    if fused:
        out_ref, *rest = rest
    else:
        att_hbm, w_out_hbm, *rest = rest
    (q_ref, k_ref, v_ref, w_ref, wbuf, att, acc, sub, outgoing, incoming, scale_out, scale_in, mixb,
     load_sem, own_sem, pair_send, pair_recv, w_send, w_recv, s_send, s_recv, t_send, t_recv, a_send, a_recv, out_v, out_sem) = rest
    me = lax.axis_index("seq")
    core = lax.axis_index("head")
    other = 1 - core
    tokens, width = q_ref.shape
    heads = width // HD
    cols = wbuf.shape[-1]
    bits = n.bit_length() - 1
    groups = a_send.shape[0]
    per = heads // groups
    place = [me // stride % length for length, stride in dims]

    loads = [
        pltpu.make_async_copy(src, dst, load_sem.at[i])
        for i, (src, dst) in enumerate(((w_hbm, w_ref), (k_hbm, k_ref), (v_hbm, v_ref), (q_hbm, q_ref)))
    ]
    for load in loads:
        load.start()

    barrier = pltpu.get_barrier_semaphore()
    total = 1
    pl.semaphore_signal(barrier, inc=1, device_id=(me, other), device_id_type=MESH)
    for bit in range(bits):
        pl.semaphore_signal(barrier, inc=1, device_id=(me ^ (1 << bit), core), device_id_type=MESH)
        total += 1
    for (length, stride), p in zip(dims, place):
        if length == 2:
            continue
        for step in (-1, 1):
            there = jnp.logical_and(p + step >= 0, p + step < length)

            @pl.when(there)
            def _():
                pl.semaphore_signal(barrier, inc=1, device_id=(me + step * stride, core), device_id_type=MESH)

            total = total + there.astype(jnp.int32)

    for l in range(bits + 1):
        if l == 0:
            ids = lax.broadcasted_iota(jnp.int32, (table_ref.shape[0], tokens), 0)
            one_hot = (ids == pattern_ref[...].reshape(1, tokens)).astype(jnp.float32)
            mix = lax.dot_general(
                one_hot, table_ref[...], (((0,), (0,)), ((), ())),
                precision=lax.Precision.HIGHEST, preferred_element_type=jnp.float32,
            )
        factor = 1.0 / math.sqrt(tokens * (1 if l == 0 else 2 ** (l - 1)))
        mixb[l] = jnp.broadcast_to(mix[:, l : l + 1] * factor, (tokens, HD))

    def head_cols(h):
        return slice(h * HD, (h + 1) * HD)

    loads[1].wait()
    loads[2].wait()

    def pack_state(level, h, state):
        top = jnp.maximum(jnp.max(jnp.abs(state), axis=0, keepdims=True), 1e-30)
        scaled = jnp.round(state * (32767.0 / top))
        outgoing[level, h] = scaled.astype(jnp.int32).astype(jnp.int16)
        scale_out[level, h] = jnp.broadcast_to(top * (1.0 / 32767.0), (8, HD))

    def unpack_state(level, h):
        return incoming[level, h].astype(jnp.int32).astype(jnp.float32) * scale_in[level, h, 0:1]

    def make_states(h):
        state = lax.dot_general(
            k_ref[:, head_cols(h)], v_ref[:, head_cols(h)], (((0,), (0,)), ((), ())),
            preferred_element_type=jnp.float32,
        )
        sub[h] = state
        pack_state(0, h, state)

    for h in range(heads):
        make_states(h)
    loads[0].wait()
    pl.semaphore_wait(barrier, total)

    def pair_copy():
        return pltpu.make_async_remote_copy(
            src_ref=w_ref.at[0, :, pl.ds(pl.multiple_of(other * cols, 128), cols)],
            dst_ref=wbuf.at[core, me], send_sem=pair_send, recv_sem=pair_recv,
            device_id=(me, other), device_id_type=MESH,
        )

    def pair_landed():
        return pltpu.make_async_remote_copy(
            src_ref=w_ref.at[0, :, pl.ds(pl.multiple_of(other * cols, 128), cols)],
            dst_ref=wbuf.at[other, me], send_sem=pair_send, recv_sem=pair_recv,
            device_id=(me, other), device_id_type=MESH,
        )

    pair_copy().start()
    own = pltpu.make_async_copy(
        w_ref.at[0, :, pl.ds(pl.multiple_of(core * cols, 128), cols)], wbuf.at[core, me], own_sem
    )
    own.start()

    def state_copy(level, group):
        piece = pl.ds(group * per, per)
        return pltpu.make_async_remote_copy(
            src_ref=outgoing.at[level, piece], dst_ref=incoming.at[level, piece],
            send_sem=s_send.at[level, group], recv_sem=s_recv.at[level, group],
            device_id=(me ^ (1 << level), core), device_id_type=MESH,
        )

    def scale_copy(level, group):
        piece = pl.ds(group * per, per)
        return pltpu.make_async_remote_copy(
            src_ref=scale_out.at[level, piece], dst_ref=scale_in.at[level, piece],
            send_sem=t_send.at[level, group], recv_sem=t_recv.at[level, group],
            device_id=(me ^ (1 << level), core), device_id_type=MESH,
        )

    def sum_needed(level):
        return me // 2 ** (level + 1) != n // 2 ** (level + 1) - 1

    def active(level):
        return me // 2**level % 2 == 1

    def sends(level):
        return jnp.logical_or(jnp.logical_not(active(level)), sum_needed(level))

    def receives(level):
        return jnp.logical_or(active(level), sum_needed(level))

    for group in range(groups):
        @pl.when(sends(0))
        def _():
            scale_copy(0, group).start()
            state_copy(0, group).start()

    def weight_copy(part, source, slot, target):
        lo, size = cuts[part]
        piece = wbuf.at[:, source, :, pl.ds(lo, size)]
        return pltpu.make_async_remote_copy(
            src_ref=piece, dst_ref=piece,
            send_sem=w_send.at[part, source if fused else 0, slot], recv_sem=w_recv.at[part, source],
            device_id=(target, core), device_id_type=MESH,
        )

    def forward(part, source, at, arrived, action):
        order = orders[part]
        for rank in range(max(arrived, 0), len(order)):
            d = order[rank]
            length, stride = dims[d]
            for slot, step in ((2 * rank, 1), (2 * rank + 1, -1)):
                if rank == arrived and length == 2:
                    continue
                ok = jnp.logical_and(place[d] + step >= 0, place[d] + step < length)
                if rank == arrived:
                    ok = jnp.logical_and(ok, (place[d] - at[d]) * step > 0)

                @pl.when(ok)
                def _():
                    copy = weight_copy(part, source, slot, me + step * stride)
                    if action == "start":
                        copy.start()
                    else:
                        copy.wait_send()

    def source_of(part, ks):
        at = {d: nearest(k, place[d], dims[d][0]) for d, k in zip(orders[part], ks)}
        return at, sum(at[d] * dims[d][1] for d in at)

    def arrived_by(ks):
        return max((r for r, k in enumerate(ks) if k), default=-1)

    def weight_event(part, ks, arrived):
        at, source = source_of(part, ks)
        weight_copy(part, source, 0, me).wait_recv()
        forward(part, source, at, arrived, "start")
        if not fused:
            forward(part, source, at, arrived, "wait")

    def read_state(level, h):
        block = unpack_state(level, h)
        high = block.astype(jnp.bfloat16)
        low = (block - high.astype(jnp.float32)).astype(jnp.bfloat16)
        query = q_ref[:, head_cols(h)]
        acc[:, head_cols(h)] += mixb[level + 1] * (
            jnp.dot(query, high, preferred_element_type=jnp.float32)
            + jnp.dot(query, low, preferred_element_type=jnp.float32)
        )

    def within_event(h):
        columns = head_cols(h)
        scores = lax.dot_general(
            q_ref[:, columns], k_ref[:, columns], (((1,), (1,)), ((), ())),
            preferred_element_type=jnp.float32,
        )
        row = lax.broadcasted_iota(jnp.int32, (tokens, tokens), 0)
        col = lax.broadcasted_iota(jnp.int32, (tokens, tokens), 1)
        inner = jnp.where(col <= row, scores, 0.0).astype(jnp.bfloat16)
        acc[:, columns] = mixb[0] * jnp.dot(inner, v_ref[:, columns], preferred_element_type=jnp.float32)

    def att_copy(group, mine):
        columns = pl.ds(group * per * HD, per * HD)
        which = core if mine else other
        return pltpu.make_async_remote_copy(
            src_ref=att.at[core, :, columns], dst_ref=att.at[which, :, columns],
            send_sem=a_send.at[group], recv_sem=a_recv.at[group],
            device_id=(me, other), device_id_type=MESH,
        )

    def state_event(level, group):
        @pl.when(receives(level))
        def _():
            scale_copy(level, group).wait_recv()
            state_copy(level, group).wait_recv()

        span = range(group * per, (group + 1) * per)
        if level + 1 < bits:
            @pl.when(sum_needed(level))
            def _():
                for h in span:
                    summed = sub[h] + unpack_state(level, h)
                    sub[h] = summed
                    pack_state(level + 1, h, summed)

            @pl.when(sends(level + 1))
            def _():
                scale_copy(level + 1, group).start()
                state_copy(level + 1, group).start()

        @pl.when(active(level))
        def _():
            for h in span:
                read_state(level, h)

        if level + 1 == bits:
            columns = slice(group * per * HD, (group + 1) * per * HD)
            att[core, :, columns] = acc[:, columns].astype(jnp.bfloat16)
            att_copy(group, True).start()

    own.wait()
    pair_landed().wait_recv()
    for part in range(len(orders)):
        at, source = source_of(part, (0,) * len(dims))
        forward(part, source, at, -1, "start")
        if not fused:
            forward(part, source, at, -1, "wait")
    loads[3].wait()

    def project(part):
        lo, size = cuts[part]
        columns = slice(lo, lo + size)
        flat = [wbuf[g, :, :, columns].reshape(-1, size) for g in range(2)]
        out_v[:, columns] = jnp.dot(att[0], flat[0], preferred_element_type=jnp.float32) + jnp.dot(
            att[1], flat[1], preferred_element_type=jnp.float32
        )

    def out_copy(part):
        columns = pl.ds(*cuts[part])
        return pltpu.make_async_copy(out_v.at[:, columns], out_ref.at[:, columns], out_sem.at[part])

    for event in events:
        if event[0] == "within":
            within_event(event[1])
        elif event[0] == "state":
            state_event(event[1], event[2])
        elif event[0] == "weight":
            weight_event(*event[1:])
        elif event[0] == "loop":
            lengths = [[dims[d][0] for d in order] for order in orders]

            def each(e, carry):
                for part, order in enumerate(orders):
                    for arrived in range(len(order)):
                        below = math.prod(lengths[part][:arrived])
                        ks = []
                        rest_e = e
                        for length in lengths[part]:
                            ks.append(rest_e % length)
                            rest_e = rest_e // length

                        @pl.when(jnp.logical_and(e >= below, e < below * lengths[part][arrived]))
                        def _():
                            weight_event(part, ks, arrived)

                return carry

            lax.fori_loop(1, n, each, 0)
        elif event[0] == "att":
            for group in range(groups):
                att_copy(group, False).wait_recv()
        elif event[0] == "project" and fused:
            project(event[1])
            out_copy(event[1]).start()

    def finish(part, e):
        ks = []
        for d in orders[part]:
            ks.append(e % dims[d][0])
            e = e // dims[d][0]
        return ks

    pair_copy().wait_send()
    for group in range(groups):
        att_copy(group, True).wait_send()
        for level in range(bits):
            @pl.when(sends(level))
            def _():
                scale_copy(level, group).wait_send()
                state_copy(level, group).wait_send()
    if fused:
        for part in range(len(orders)):
            for e in range(n):
                ks = finish(part, e)
                at, source = source_of(part, ks)
                forward(part, source, at, arrived_by(ks), "wait")
    if fused:
        for part in range(len(orders)):
            out_copy(part).wait()
    else:
        stores = [pltpu.make_async_copy(att, att_hbm, load_sem.at[0]), pltpu.make_async_copy(wbuf, w_out_hbm, load_sem.at[1])]
        for store in stores:
            store.start()
        for store in stores:
            store.wait()


def schedule(dims, orders, cuts, n, heads, groups, unrolled):
    bits = n.bit_length() - 1
    whole = sum(size for _, size in cuts)
    timed = []
    for h in range(heads):
        timed.append((0.35 * h / heads, ("within", h)))
    for level in range(bits):
        for group in range(groups):
            timed.append((0.45 + 0.75 * level + 0.25 * group, ("state", level, group)))
    if not unrolled:
        tail = [("loop",), ("att",)]
    else:
        last = {}
        for part, order in enumerate(orders):
            lengths = [dims[d][0] for d in order]
            count = [0] * len(order)
            for rev in itertools.product(*[range(length) for length in lengths[::-1]]):
                ks = rev[::-1]
                arrived = max((r for r, k in enumerate(ks) if k), default=-1)
                if arrived < 0:
                    continue
                count[arrived] += 1
                when = count[arrived] * cuts[part][1] / whole * 1.8 + 0.3 * sum(1 for k in ks if k)
                if arrived == len(order) - 1 and lengths[-1] == 2:
                    when += 100
                timed.append((when, ("weight", part, ks, arrived)))
        tail = [("att",)]
    timed.sort(key=lambda t: t[0])
    return [e for _, e in timed] + tail + [("project", p) for p in range(len(orders))]


def on_device(dims, queries, keys, values, level_pattern, level_weight, out_weight):
    n = lax.axis_size("seq")
    tokens, width = queries.shape
    heads = width // HD
    bits = n.bit_length() - 1
    _, rows, full = out_weight.shape
    cols = full // 2
    fused = rows % 16 == 0
    groups = min(4, heads)
    tiles = cols // 128
    if len(dims) == 3:
        long = max(range(3), key=lambda i: dims[i][0])
        a, b = [i for i in range(3) if i != long]
        orders = [(long, a, b), (long, b, a), (a, b, long)]
        share = max(1, tiles * 3 // 8)
        sizes = [share, share, tiles - 2 * share]
    else:
        orders, sizes = [tuple(range(len(dims)))], [tiles]
    cuts, lo = [], 0
    for size in sizes:
        cuts.append((lo * 128, size * 128))
        lo += size
    events = schedule(dims, orders, cuts, n, heads, groups, fused)
    plan = (dims, orders, cuts, events, n, fused)
    bf16, f32 = jnp.bfloat16, jnp.float32
    any_spec = pl.BlockSpec(memory_space=pl.ANY)
    vmem_spec = pl.BlockSpec(memory_space=pltpu.VMEM)
    if fused:
        out_shape = jax.ShapeDtypeStruct((tokens, cols), f32)
        out_specs = any_spec
    else:
        out_shape = [
            jax.ShapeDtypeStruct((2, tokens, width), bf16),
            jax.ShapeDtypeStruct((2, n, rows, cols), bf16),
        ]
        out_specs = [any_spec, any_spec]
    dma = pltpu.SemaphoreType.DMA
    result = pl.pallas_call(
        functools.partial(kernel, plan),
        out_shape=out_shape,
        in_specs=[any_spec] * 3 + [vmem_spec] * 2 + [any_spec],
        out_specs=out_specs,
        scratch_shapes=[
            pltpu.VMEM((tokens, width), bf16),
            pltpu.VMEM((tokens, width), bf16),
            pltpu.VMEM((tokens, width), bf16),
            pltpu.VMEM((1, rows, full), bf16),
            pltpu.VMEM((2, n, rows, cols), bf16),
            pltpu.VMEM((2, tokens, width), bf16),
            pltpu.VMEM((tokens, width), f32),
            pltpu.VMEM((heads, HD, HD), f32),
            pltpu.VMEM((bits, heads, HD, HD), jnp.int16),
            pltpu.VMEM((bits, heads, HD, HD), jnp.int16),
            pltpu.VMEM((bits, heads, 8, HD), f32),
            pltpu.VMEM((bits, heads, 8, HD), f32),
            pltpu.VMEM((bits + 1, tokens, HD), f32),
            dma((4,)),
            dma,
            dma,
            dma,
            dma((len(orders), n if fused else 1, 2 * len(dims))),
            dma((len(orders), n)),
            dma((bits, groups)),
            dma((bits, groups)),
            dma((bits, groups)),
            dma((bits, groups)),
            dma((groups,)),
            dma((groups,)),
            pltpu.VMEM((tokens, cols) if fused else (8, 128), f32),
            dma((len(orders),)),
        ],
        compiler_params=pltpu.CompilerParams(
            collective_id=0, has_side_effects=True, vmem_limit_bytes=60 * 2**20
        ),
    )(queries, keys, values, level_pattern, level_weight, out_weight)
    if fused:
        return result
    att, gathered = result
    return jnp.einsum(
        "gtk,gkd->td", att, gathered.reshape(2, n * rows, cols), preferred_element_type=f32
    )


def solution(mesh):
    placed = (
        P("seq", "head"),
        P("seq", "head"),
        P("seq", "head"),
        P("seq"),
        P(),
        P("head", "seq", None),
    )
    return jax.shard_map(
        functools.partial(on_device, line_dims(mesh)),
        mesh=mesh, in_specs=placed, out_specs=P("seq", "head"), check_vma=False,
    )
```
